32 devices in a mesh: row: 4 (over y, core), col: 8 (over z, x).
Axes of the slice: x: 2, y: 2, z: 4, core: 2. Of those that a mesh axis runs over, the one named last changes fastest.
Arguments:
- weight: bfloat16 [8192, 16384], P('row', 'col'), may hold values from -3 to 3
- momentum: float32 [8192, 16384], P('row', 'col'), may hold values from -100 to 100, as said below
- gradient: bfloat16 [8192, 16384], P('row', 'col'), may hold values from -6 to 6
- prev_basis: bfloat16 [16384, 512], P('col'), may hold values from -6 to 6
Outputs:
- new_weight: bfloat16 [8192, 16384], P('row', 'col')
- new_momentum: float32 [8192, 16384], P('row', 'col')
- new_basis: bfloat16 [16384, 512], P('col')
The draws below stay inside these ranges and needn't reach their ends.
Inputs may be any that keep to these rules, and one draw needn't show every extreme that they name: momentum has rows and columns of different scales.
All inputs are finite; a program needn't handle non-finite values.
Results may differ from the reference program's by a relative error of at most 0.0021.
Values may be sent and summed in bfloat16 or wider, within the bound.
No kernel may reach another device: no remote copies, remote signals or barrier semaphores. Data moves between devices by JAX's collectives and lax.ppermute only.
A program may use at most 128 MiB of HBM per device.

```python
import jax
import jax.numpy as jnp
from jax import lax

M = 8192
N = 16384
R = 512
COLS_DEV = 2048


def draw_momentum(key, part):
    row_key = jax.random.fold_in(key, 11)
    col_key = jax.random.fold_in(key, 12)
    entry_key = jax.random.fold_in(key, 13)
    positions = jnp.arange(N, dtype=jnp.float32) / N
    inside = (jnp.arange(N, dtype=jnp.int32) % COLS_DEV).astype(jnp.float32) / COLS_DEV
    spread = jax.random.uniform(col_key, (N,), jnp.float32)
    row_scale = 10.0 ** jax.random.uniform(row_key, (M, 1), jnp.float32)
    col_power = 0.3 * spread + 0.3 * positions + 0.5 * inside
    entries = jnp.clip(jax.random.normal(entry_key, (M, N), jnp.float32), -6.0, 6.0)
    col_scale = (10.0 ** col_power)[None, :]
    return entries * row_scale * col_scale / 20.0


def block_levels(key, extent, cuts, smallest, top_value):
    level = 1.0
    for position, blocks in cuts:
        draws = jax.random.uniform(jax.random.fold_in(jax.random.fold_in(key, 6), position), (blocks,), jnp.float32, smallest / len(cuts), top_value / len(cuts))
        level = level * jnp.repeat(jnp.exp(draws), extent[position] // blocks).reshape((-1,) + (1,) * (len(extent) - 1 - position))
    return level


def scatter_about(stream_key, extent, deviation, limit, split=(), kind=jnp.bfloat16):
    factor_of = block_levels(stream_key, extent, split, -0.22, 0.18) if split else 1.0
    drawn = jax.random.normal(stream_key, extent, jnp.float32) * deviation * factor_of
    return jnp.minimum(jnp.maximum(drawn, -limit), limit).astype(kind)


def setup_inputs(seed: int = 0) -> dict:
    splits = jax.random.split(jax.random.key(seed), 5)
    weight = scatter_about(splits[0], (M, N), 0.5, 3.0, ((0, 4), (1, 8)))
    momentum = draw_momentum(jax.random.fold_in(splits[4], 71), 0)
    gradient = scatter_about(splits[2], (M, N), 1.0, 6.0, ((0, 4), (1, 8)))
    prev_basis = scatter_about(splits[3], (N, R), 1.0, 6.0, ((0, 8),))
    return {"weight": weight, "momentum": momentum, "gradient": gradient, "prev_basis": prev_basis}


decay_loss = 0.1
step_size = 0.4
epsilon = 1e-06

def reference(weight, momentum, gradient, prev_basis):
    high = lax.Precision.HIGHEST
    buffer = momentum + gradient.astype(jnp.float32)
    left_factor = jnp.dot(buffer, prev_basis.astype(jnp.float32), precision=high)
    gram_matrix = jnp.dot(left_factor.T, left_factor, precision=high)
    lower_tri = jnp.linalg.cholesky(gram_matrix)
    orthonormal = jax.scipy.linalg.solve_triangular(lower_tri, left_factor.T, lower=True).T
    right_factor = jnp.dot(buffer.T, orthonormal, precision=high)
    column_scale = jnp.sqrt(lax.optimization_barrier(jnp.sum(right_factor * right_factor, axis=0)) / N + epsilon)
    new_basis = (right_factor / column_scale).astype(jnp.bfloat16)
    basis_float = new_basis.astype(jnp.float32)
    new_momentum = buffer - decay_loss * jnp.dot(orthonormal * column_scale, basis_float.T, precision=high)
    update = jnp.dot(orthonormal, basis_float.T, precision=high)
    new_weight = (weight.astype(jnp.float32) - step_size * (M / N) ** 0.5 * update).astype(jnp.bfloat16)
    return (new_weight, new_momentum, new_basis)
```

```python
import functools
import jax
import jax.numpy as jnp
from jax import lax
from jax.experimental import pallas as pl
from jax.experimental.pallas import tpu as pltpu
from jax.sharding import PartitionSpec as P

HI = lax.Precision.HIGHEST
F32 = jnp.float32
NB = 128
G = 8


def factor_block(d, x):
    n = len(d)
    for b in range(n):
        own = d[b]
        cols = [jnp.broadcast_to(own[:, G * b + k : G * b + k + 1], (G, NB)) for k in range(G)]
        s = {}
        for i in range(G):
            for k in range(i + 1):
                s[i, k] = jnp.broadcast_to(cols[k][i : i + 1, :], (G, NB))
        inv = []
        low = {}
        for k in range(G):
            r = 1.0 / s[k, k]
            inv.append(r)
            for i in range(k + 1, G):
                low[i, k] = s[i, k] * r
            for i in range(k + 1, G):
                for j in range(k + 1, i + 1):
                    s[i, j] = s[i, j] - low[i, k] * s[j, k]
        rows = [
            [jnp.broadcast_to(m[k : k + 1, :], (G, NB)) for k in range(G)] for m in (own, x[b])
        ]
        for part in rows:
            for i in range(1, G):
                for k in range(i):
                    part[i] = part[i] - low[i, k] * part[k]
        sub = lax.broadcasted_iota(jnp.int32, (G, NB), 0)
        out = jnp.zeros((G, NB), F32)
        for k in range(G):
            out = jnp.where(sub == k, rows[1][k] * lax.rsqrt(s[k, k]), out)
        z = []
        for part in rows:
            t = [part[k] * inv[k] for k in range(G)]
            for k in range(G - 2, -1, -1):
                for i in range(k + 1, G):
                    t[k] = t[k] - low[i, k] * t[i]
            z.append(t)
        for g in range(b + 1, n):
            col = [jnp.broadcast_to(d[g][:, G * b + k : G * b + k + 1], (G, NB)) for k in range(G)]
            dd = [col[k] * z[0][k] for k in range(G)]
            xx = [col[k] * z[1][k] for k in range(G)]
            while len(dd) > 1:
                dd = [dd[i] + dd[i + 1] for i in range(0, len(dd), 2)]
                xx = [xx[i] + xx[i + 1] for i in range(0, len(xx), 2)]
            d[g] = d[g] - dd[0]
            x[g] = x[g] - xx[0]
        x[b] = out
    return x


def chol_kernel(g_ref, y_ref, a_ref, xb_ref):
    rank = g_ref.shape[0]
    nb = rank // NB
    a_ref[...] = g_ref[...]
    ri = lax.broadcasted_iota(jnp.int32, (rank, rank), 0)
    ci = lax.broadcasted_iota(jnp.int32, (rank, rank), 1)
    y_ref[...] = jnp.where(ri == ci, 1.0, 0.0).astype(F32)

    @pl.loop(0, nb)
    def _(p):
        at = pl.multiple_of(p * NB, NB)
        d = [a_ref[pl.ds(pl.multiple_of(at + G * i, G), G), pl.ds(at, NB)] for i in range(NB // G)]
        sub = lax.broadcasted_iota(jnp.int32, (G, NB), 0)
        lane = lax.broadcasted_iota(jnp.int32, (G, NB), 1)
        x = [jnp.where(lane == sub + G * i, 1.0, 0.0).astype(F32) for i in range(NB // G)]
        x = factor_block(d, x)
        for i in range(NB // G):
            xb_ref[pl.ds(G * i, G), :] = x[i]
        for q in range(nb):

            @pl.when(p == q)
            def _():
                s0, s1 = q * NB, (q + 1) * NB
                xb = xb_ref[...]
                if q:
                    y_ref[s0:s1, :s0] = jnp.dot(xb, y_ref[s0:s1, :s0], precision=HI)
                y_ref[s0:s1, s0:s1] = xb
                if q < nb - 1:
                    up = jnp.dot(xb, a_ref[s0:s1, s1:], precision=HI)
                    both = jnp.concatenate([up, y_ref[s0:s1, :s1]], axis=1)
                    upd = lax.dot_general(up, both, (((0,), (0,)), ((), ())), precision=HI)
                    w = rank - s1
                    a_ref[s1:, s1:] = a_ref[s1:, s1:] - upd[:, :w]
                    y_ref[s1:, :s1] = y_ref[s1:, :s1] - upd[:, w:]


def chol_inverse(g):
    rank = g.shape[0]
    return pl.pallas_call(
        chol_kernel,
        out_shape=jax.ShapeDtypeStruct((rank, rank), F32),
        scratch_shapes=[pltpu.VMEM((rank, rank), F32), pltpu.VMEM((NB, NB), F32)],
        name="chol",
    )(g)


BF16 = jnp.bfloat16
decay_loss = 0.1
step_size = 0.4
epsilon = 1e-06
CHUNKS = 4
TILE = 256
PARAMS = pltpu.CompilerParams(vmem_limit_bytes=56 * 2**20)


def halves(v):
    hi = v.astype(BF16)
    return hi, (v - hi.astype(F32)).astype(BF16)


def dot(a, b, dims=((1,), (0,))):
    return lax.dot_general(a, b, (dims, ((), ())), preferred_element_type=F32)


def dot3(a, b, dims=((1,), (0,))):
    ah, al = halves(a)
    bh, bl = halves(b)
    return dot(ah, bh, dims) + (dot(al, bh, dims) + dot(ah, bl, dims))


def left_kernel(m_ref, g_ref, q_ref, o_ref):
    hi, lo = halves(m_ref[...] + g_ref[...].astype(F32))
    o_ref[...] = dot(hi, q_ref[...]) + dot(lo, q_ref[...])


def left_chunk(momentum, gradient, basis, chunk):
    rows, cols = momentum.shape
    rank = basis.shape[1]
    steps = rows // CHUNKS // TILE
    tile = pl.BlockSpec((TILE, cols), lambda i: (chunk * steps + i, 0))
    return pl.pallas_call(
        left_kernel,
        grid=(steps,),
        in_specs=[tile, tile, pl.BlockSpec((cols, rank), lambda i: (0, 0))],
        out_specs=pl.BlockSpec((TILE, rank), lambda i: (i, 0)),
        out_shape=jax.ShapeDtypeStruct((rows // CHUNKS, rank), F32),
        compiler_params=PARAMS,
        name="left",
    )(momentum, gradient, basis)


def gram_kernel(l_ref, o_ref):
    @pl.when(pl.program_id(0) == 0)
    def _():
        o_ref[...] = jnp.zeros_like(o_ref)

    part = l_ref[...]
    o_ref[...] += lax.dot_general(part, part, (((0,), (0,)), ((), ())), precision=HI)


def gram(left):
    rows, rank = left.shape
    return pl.pallas_call(
        gram_kernel,
        grid=(rows // TILE,),
        in_specs=[pl.BlockSpec((TILE, rank), lambda i: (i, 0))],
        out_specs=pl.BlockSpec((rank, rank), lambda i: (0, 0)),
        out_shape=jax.ShapeDtypeStruct((rank, rank), F32),
        compiler_params=PARAMS,
        name="gram",
    )(left)


def back_kernel(m_ref, g_ref, l_ref, o_ref):
    @pl.when(pl.program_id(0) == 0)
    def _():
        o_ref[...] = jnp.zeros_like(o_ref)

    o_ref[...] += dot3(l_ref[...], m_ref[...] + g_ref[...].astype(F32), ((0,), (0,)))


def back(momentum, gradient, left):
    rows, cols = momentum.shape
    rank = left.shape[1]
    tile = pl.BlockSpec((TILE, cols), lambda i: (i, 0))
    return pl.pallas_call(
        back_kernel,
        grid=(rows // TILE,),
        in_specs=[tile, tile, pl.BlockSpec((TILE, rank), lambda i: (i, 0))],
        out_specs=pl.BlockSpec((rank, cols), lambda i: (0, 0)),
        out_shape=jax.ShapeDtypeStruct((rank, cols), F32),
        compiler_params=PARAMS,
        name="back",
    )(momentum, gradient, left)


def right_kernel(y_ref, w_ref, r_ref, s_ref):
    r = dot3(y_ref[...], w_ref[...])
    r_ref[...] = r
    total = jnp.sum(r * r, axis=1, keepdims=True)
    s_ref[...] = jnp.broadcast_to(total, s_ref.shape)


def right(inverse, back_sum):
    rank, cols = back_sum.shape
    return pl.pallas_call(
        right_kernel,
        out_shape=(
            jax.ShapeDtypeStruct((rank, cols), F32),
            jax.ShapeDtypeStruct((rank, 128), F32),
        ),
        compiler_params=PARAMS,
        name="right",
    )(inverse, back_sum)


def ortho_kernel(l_ref, y_ref, o_ref):
    o_ref[...] = dot3(l_ref[...], y_ref[...], ((1,), (1,)))


def ortho(left, inverse):
    rows, rank = left.shape
    tile = pl.BlockSpec((TILE, rank), lambda i: (i, 0))
    return pl.pallas_call(
        ortho_kernel,
        grid=(rows // TILE,),
        in_specs=[tile, pl.BlockSpec((rank, rank), lambda i: (0, 0))],
        out_specs=tile,
        out_shape=jax.ShapeDtypeStruct((rows, rank), F32),
        compiler_params=PARAMS,
        name="ortho",
    )(left, inverse)


def final_kernel(
    update_scale, w_ref, m_ref, g_ref, o_ref, r_ref, sc_ref, sr_ref, nw_ref, nm_ref, nb_ref, n_ref
):
    @pl.when(pl.program_id(0) == 0)
    def _():
        basis = r_ref[...] / sc_ref[...][:, :1]
        n_ref[...] = basis.astype(BF16)
        nb_ref[...] = basis.T.astype(BF16)

    basis = n_ref[...]
    ortho_part = o_ref[...]
    hi, lo = halves(ortho_part)
    scaled = (ortho_part * sr_ref[...][:1, :]).astype(BF16)
    nm_ref[...] = m_ref[...] + g_ref[...].astype(F32) - decay_loss * dot(scaled, basis)
    update = dot(hi, basis) + dot(lo, basis)
    nw_ref[...] = (w_ref[...].astype(F32) - update_scale * update).astype(BF16)


def final(update_scale, weight, momentum, gradient, orthonormal, right_t, scale):
    rows, cols = momentum.shape
    rank = orthonormal.shape[1]
    tile = pl.BlockSpec((TILE, cols), lambda i: (i, 0))
    whole = lambda a: pl.BlockSpec(a.shape, lambda i: (0, 0))
    row = jnp.broadcast_to(scale[:, 0][None, :], (8, rank))
    return pl.pallas_call(
        functools.partial(final_kernel, update_scale),
        grid=(rows // TILE,),
        in_specs=[
            tile,
            tile,
            tile,
            pl.BlockSpec((TILE, rank), lambda i: (i, 0)),
            whole(right_t),
            whole(scale),
            whole(row),
        ],
        out_specs=(tile, tile, pl.BlockSpec((cols, rank), lambda i: (0, 0))),
        out_shape=(
            jax.ShapeDtypeStruct((rows, cols), BF16),
            jax.ShapeDtypeStruct((rows, cols), F32),
            jax.ShapeDtypeStruct((cols, rank), BF16),
        ),
        scratch_shapes=[pltpu.VMEM((rank, cols), BF16)],
        compiler_params=PARAMS,
        name="final",
    )(weight, momentum, gradient, orthonormal, right_t, scale, row)


def swap(v, axis, size, bit):
    return lax.ppermute(v, axis, [(i, i ^ (1 << bit)) for i in range(size)])


def side(axis, bit):
    return (lax.axis_index(axis) >> bit) & 1


def halve(v, axis, size, bit):
    half = v.shape[0] // 2
    mine = side(axis, bit)
    send = lax.dynamic_slice_in_dim(v, (1 - mine) * half, half)
    keep = lax.dynamic_slice_in_dim(v, mine * half, half)
    return keep + swap(send, axis, size, bit)


def double(v, axis, size, bit):
    other = swap(v, axis, size, bit)
    half = v.shape[0]
    mine = side(axis, bit)
    out = jnp.zeros((2 * half,) + v.shape[1:], v.dtype)
    out = lax.dynamic_update_slice_in_dim(out, v, mine * half, 0)
    return lax.dynamic_update_slice_in_dim(out, other, (1 - mine) * half, 0)


def bits(size):
    return range(size.bit_length() - 1)


def per_device(mesh, weight, momentum, gradient, prev_basis):
    rows, cols = mesh.shape["row"], mesh.shape["col"]
    total_rows, total_cols = momentum.shape[0] * rows, momentum.shape[1] * cols
    pieces = []
    for chunk in range(CHUNKS):
        part = left_chunk(momentum, gradient, prev_basis, chunk)
        for bit in bits(cols):
            part = halve(part, "col", cols, bit)
        pieces.append(part)
    chunks = []
    for part in pieces:
        for bit in reversed(bits(cols)):
            part = double(part, "col", cols, bit)
        chunks.append(part)
    left = jnp.concatenate(chunks)

    gram_matrix = halve(gram(left), "row", rows, 0)
    back_sum = halve(back(momentum, gradient, left), "row", rows, 0)
    for bit in bits(rows)[1:]:
        gram_matrix = gram_matrix + swap(gram_matrix, "row", rows, bit)
        back_sum = back_sum + swap(back_sum, "row", rows, bit)
    gram_matrix = double(gram_matrix, "row", rows, 0)
    back_sum = double(back_sum, "row", rows, 0)

    inverse = chol_inverse(gram_matrix)
    right_t, square_sum = right(inverse, back_sum)
    for bit in bits(cols):
        square_sum = square_sum + swap(square_sum, "col", cols, bit)
    orthonormal = ortho(left, inverse)
    scale = jnp.sqrt(square_sum / total_cols + epsilon)
    update_scale = step_size * (total_rows / total_cols) ** 0.5
    return final(update_scale, weight, momentum, gradient, orthonormal, right_t, scale)


def solution(mesh):
    return jax.shard_map(
        functools.partial(per_device, mesh),
        mesh=mesh,
        in_specs=(P("row", "col"), P("row", "col"), P("row", "col"), P("col", None)),
        out_specs=(P("row", "col"), P("row", "col"), P("col", None)),
        check_vma=False,
    )
```
